32 devices in a mesh: pulse: 8 (over z, core), range: 4 (over y, x).
Axes of the slice: x: 2, y: 2, z: 4, core: 2. Of those that a mesh axis runs over, the one named last changes fastest.
Arguments:
- echoes: bfloat16 [2, 2048, 4096], P(None, 'pulse', 'range'), may hold values from -6 to 6
- chirp: bfloat16 [2, 128], replicated, may hold values from -0.375 to 0.375
- beam_weights: bfloat16 [2048, 512], P('pulse'), may hold values from -0.25 to 0.25
- merge_weights: bfloat16 [3, 2, 2, 2048, 256], P(None, None, None, 'pulse'), may hold values from -0.1875 to 0.1875
- range_offsets: int32 [3, 2048], P(None, 'pulse'), may hold values from -8 to 8
Outputs:
- focused: bfloat16 [4096, 4096], P('range', 'pulse')
The draws below stay inside these ranges and needn't reach their ends.
All inputs are finite; a program needn't handle non-finite values.
Results may differ from the reference program's by a relative error of at most 0.0075.
Values may be sent and summed in bfloat16 or wider, within the bound.
No kernel may reach another device: no remote copies, remote signals or barrier semaphores. Data moves between devices by JAX's collectives and lax.ppermute only.
A program may use at most 64 MiB of HBM per device.

```python
import jax
import jax.numpy as jnp
from jax import lax

TAPS = 128
P_DEV = 256
B = 256
MAXOFF = 8
LEVELS = 3
PULSES = 2048
NR = 4096
N_PULSE = 8


def with_ends(result, key, low, high):
    longest = result.shape.index(max(result.shape))
    spots = []
    for shift in (0, 1):
        where = [jax.random.randint(jax.random.fold_in(key, axis), (), 0, length) for axis, length in enumerate(result.shape)]
        where[longest] = (where[longest] + shift) % result.shape[longest]
        spots.append(tuple(where))
    return result.at[spots[0]].set(low).at[spots[1]].set(high)


def level_of(rng, dims, pieces, low, top_value):
    loudness, own = 1.0, jax.random.fold_in(rng, 6)
    for axis_at, parts in pieces:
        draws = jnp.exp(jax.random.uniform(jax.random.fold_in(own, axis_at), (parts,), jnp.float32, low / len(pieces), top_value / len(pieces)))
        loudness = loudness * jnp.repeat(draws, dims[axis_at] // parts).reshape([-1 if axis == axis_at else 1 for axis in range(len(dims))])
    return loudness


def noise(rng, extent, width, limit, pieces=(), kind=jnp.bfloat16):
    drawn = width * jax.random.normal(rng, extent, jnp.float32)
    if pieces:
        drawn = drawn * level_of(rng, extent, pieces, -0.22, 0.18)
    return jnp.clip(drawn, -limit, limit).astype(kind)


def setup_inputs(seed: int = 0) -> dict:
    key_list = jax.random.split(jax.random.key(seed), 6)
    echoes = noise(key_list[0], (2, PULSES, NR), 1.0, 6.0, ((1, 8), (2, 4)))
    chirp = noise(key_list[1], (2, TAPS), (2 * TAPS) ** -0.5, 0.375)
    beam_weights = noise(key_list[2], (PULSES, 2 * B), (2 * P_DEV) ** -0.5, 0.25, ((0, 8),))
    merge_weights = noise(key_list[3], (LEVELS, 2, 2, N_PULSE * B, B), (4 * B) ** -0.5, 0.1875, ((3, 8),))
    range_offsets = with_ends(jax.random.randint(key_list[4], (LEVELS, N_PULSE * B), 0 - MAXOFF, MAXOFF + 1), jax.random.fold_in(key_list[4], 1), 0 - MAXOFF, MAXOFF).astype(jnp.int32)
    return dict(echoes=echoes, chirp=chirp, beam_weights=beam_weights, merge_weights=merge_weights, range_offsets=range_offsets)


def expand_complex(real_part, imag_part):
    upper_rows = jnp.concatenate([real_part, imag_part], axis=1)
    lower_rows = jnp.concatenate([-imag_part, real_part], axis=1)
    return jnp.concatenate([upper_rows, lower_rows], axis=0)


def replica_matrix(chirp):
    tap_count = chirp.shape[1]
    source = jnp.arange(2 * tap_count, dtype=jnp.int32)[:, None]
    target = jnp.arange(tap_count, dtype=jnp.int32)[None, :]
    lag_index = source - target
    inside_band = (lag_index >= 0) & (lag_index < tap_count)
    clipped = jnp.clip(lag_index, 0, tap_count - 1)
    replica_real = jnp.where(inside_band, chirp[0][clipped], 0).astype(chirp.dtype)
    replica_imag = jnp.where(inside_band, chirp[1][clipped], 0).astype(chirp.dtype)
    first_half = jnp.concatenate([replica_real, -replica_imag], axis=1)
    second_half = jnp.concatenate([replica_imag, replica_real], axis=1)
    return jnp.stack([first_half, second_half])


def compress(echo_block, next_rim, matrix):
    pulse_count = echo_block.shape[1]
    row_count = echo_block.shape[2]
    tap_count = next_rim.shape[2]
    extended = jnp.concatenate([echo_block, next_rim], axis=2)
    blocks = extended.reshape(2, pulse_count, row_count // tap_count + 1, tap_count)
    windows = jnp.concatenate([blocks[:, :, :-1], blocks[:, :, 1:]], axis=3)
    product = jnp.einsum("qmjs,qsn->mjn", windows.astype(jnp.float32), matrix.astype(jnp.float32),
                         precision=lax.Precision.HIGHEST)
    product = product.astype(jnp.bfloat16)
    real_rows = product[:, :, :tap_count].reshape(pulse_count, row_count)
    imag_rows = product[:, :, tap_count:].reshape(pulse_count, row_count)
    return jnp.concatenate([real_rows, imag_rows], axis=0)


def beamform(stacked, weights):
    beam_count = weights.shape[1] // 2
    expanded = expand_complex(weights[:, :beam_count], weights[:, beam_count:])
    polar = lax.dot_general(stacked.astype(jnp.float32), expanded.astype(jnp.float32),
                            (((0,), (0,)), ((), ())), precision=lax.Precision.HIGHEST)
    return polar.astype(jnp.bfloat16)


def reference(echoes, chirp, beam_weights, merge_weights, range_offsets):
    slot_count = N_PULSE
    bin_count = NR
    beam_count = B
    pulse_count = P_DEV
    matrix = replica_matrix(chirp)
    slot_ids = jnp.arange(slot_count, dtype=jnp.int32)

    def first_image(slot_index):
        echo_block = lax.dynamic_slice_in_dim(echoes, slot_index * pulse_count, pulse_count, 1)
        zero_rim = jnp.zeros((2, pulse_count, TAPS), echoes.dtype)
        stacked = compress(echo_block, zero_rim, matrix)
        weights = lax.dynamic_slice_in_dim(beam_weights, slot_index * pulse_count, pulse_count, 0)
        return beamform(stacked, weights)

    images = lax.map(first_image, slot_ids)
    for merge_step in range(LEVELS):
        level_bit = 1 << merge_step
        offsets = range_offsets[merge_step].reshape(slot_count, beam_count)
        columns = jnp.concatenate([offsets, offsets], axis=1)
        padded = jnp.pad(images, ((0, 0), (MAXOFF, MAXOFF), (0, 0)))

        def shift_one(pair_args):
            padded_block, column_shift = pair_args
            row_index = jnp.arange(bin_count, dtype=jnp.int32)[:, None] + MAXOFF + column_shift[None, :]
            return jnp.take_along_axis(padded_block, row_index.astype(jnp.int32), axis=0)

        shifted = lax.map(shift_one, (padded, columns))
        level_weights = merge_weights[merge_step].reshape(2, 2, slot_count, beam_count, beam_count)

        def merge_one(slot_index):
            lower_slot = jnp.bitwise_and(slot_index, jnp.int32(~level_bit))
            upper_slot = jnp.bitwise_or(slot_index, jnp.int32(level_bit))
            summed = jnp.zeros((bin_count, 2 * beam_count), jnp.float32)
            for which, child_slot in ((0, lower_slot), (1, upper_slot)):
                weights = level_weights[which, :, slot_index]
                expanded = expand_complex(weights[0], weights[1])
                summed = summed + jnp.dot(shifted[child_slot].astype(jnp.float32), expanded.astype(jnp.float32),
                                          precision=lax.Precision.HIGHEST)
            return summed.astype(jnp.bfloat16)

        images = lax.map(merge_one, slot_ids)
    return images.transpose(1, 0, 2).reshape(bin_count, slot_count * 2 * beam_count)
```

```python
import functools

import jax
import jax.numpy as jnp
from jax import lax
from jax.experimental import pallas as pl
from jax.experimental.pallas import tpu as pltpu
from jax.sharding import PartitionSpec as P

MAXOFF = 8
LANES = 128
F32 = jnp.float32
BF16 = jnp.bfloat16


def mm(a, b):
    return lax.dot_general(a, b, (((1,), (0,)), ((), ())), preferred_element_type=F32)


def mm_nt(a, b):
    return lax.dot_general(a, b, (((1,), (1,)), ((), ())), preferred_element_type=F32)


def mask_outside(x_ref, left, right):
    rows = x_ref.shape[0]
    if left:
        keep = jnp.full((left, x_ref.shape[1]), lax.axis_index("range"), jnp.int32) > 0
        x_ref[:left, :] = jnp.where(keep, x_ref[:left, :], 0.0)
    if right:
        last = lax.axis_size("range") - 1
        keep = jnp.full((right, x_ref.shape[1]), lax.axis_index("range"), jnp.int32) < last
        x_ref[rows - right :, :] = jnp.where(keep, x_ref[rows - right :, :], 0.0)


def shift_into(x_ref, first, offsets, out_ref):
    rows, width = out_ref.shape
    spot = lax.broadcasted_iota(jnp.int32, (8, width), 0) + MAXOFF + offsets
    index = spot & 7
    low, high = spot < 8, spot >= 16

    def turned(start):
        tile = x_ref[pl.ds(pl.multiple_of(start, 8), 8), :]
        return jnp.take_along_axis(tile, index, axis=0, mode="promise_in_bounds")

    def step(j, held):
        a, b = held
        base = first + 8 + j * 16
        c, d = turned(base), turned(base + 8)
        upper = jnp.where(low, a, jnp.where(high, c, b))
        lower = jnp.where(low, b, jnp.where(high, d, c))
        out = jnp.concatenate([upper, lower], axis=0).astype(BF16)
        out_ref[pl.ds(pl.multiple_of(j * 16, 16), 16), :] = out
        return c, d

    lax.fori_loop(0, rows // 16, step, (turned(first - 8), turned(first)), unroll=2)


def both_halves(row):
    return jnp.concatenate([row, row], axis=1)


def prepare_kernel(chirp_ref, weights_ref, band_ref, turned_ref):
    taps = chirp_ref.shape[1]
    row = lax.broadcasted_iota(jnp.int32, (taps, 2 * taps), 0)
    for part in range(2):
        line = chirp_ref[part : part + 1, :].astype(F32)
        line = jnp.concatenate([line, jnp.zeros_like(line)], axis=1)
        band = jnp.broadcast_to(line, (taps, 2 * taps))
        apart = 1
        while apart < taps:
            band = jnp.where((row & apart) != 0, pltpu.roll(band, apart, 1), band)
            apart *= 2
        band_ref[part * taps : (part + 1) * taps, :] = band.astype(BF16)
    turned_ref[...] = weights_ref[...].astype(F32).T.astype(BF16)


def prepare(chirp, weights):
    taps = chirp.shape[1]
    return pl.pallas_call(
        prepare_kernel,
        out_shape=(
            jax.ShapeDtypeStruct((2 * taps, 2 * taps), BF16),
            jax.ShapeDtypeStruct(weights.shape[::-1], BF16),
        ),
        name="prepare",
    )(chirp, weights)


def first_kernel(pieces, rows, halo, keep, edges, *refs):
    sources = refs[:-8]
    band_ref, weights_ref, offsets_ref, out_ref, echo, beams, image, sems = refs[-8:]
    copies, at = [], 0
    for n, (source, start, count) in enumerate(pieces):
        copy = pltpu.make_async_copy(
            sources[source].at[:, :, pl.ds(start, count)], echo.at[:, :, pl.ds(at, count)], sems.at[n]
        )
        copy.start()
        copies.append(copy)
        at += count
    for copy in copies:
        copy.wait()
    width = weights_ref.shape[0] // 2
    taps = band_ref.shape[0] // 2
    on_real = mm(weights_ref[...], echo[0])
    on_imag = mm(weights_ref[...], echo[1])
    beams[:width, :] = (on_real[:width] - on_imag[width:]).astype(BF16)
    beams[width:, :] = (on_real[width:] + on_imag[:width]).astype(BF16)
    inner = rows - 2 * halo
    spans = [(0, taps - halo, halo)]
    spans += [(taps * (1 + k), 0, taps) for k in range(inner // taps)]
    spans += [(taps + inner, 0, halo)]
    at = 0
    for lane, row, count in spans:
        band = jnp.concatenate([band_ref[row : row + count, :], band_ref[taps + row : taps + row + count, :]], axis=0)
        real = mm_nt(band, beams[:width, lane : lane + 2 * taps])
        imag = mm_nt(band, beams[width:, lane : lane + 2 * taps])
        image[at : at + count, :width] = real[:count] + imag[count:]
        image[at : at + count, width:] = imag[:count] - real[count:]
        at += count
    mask_outside(image, halo if "left" in edges else 0, halo if "right" in edges else 0)
    shift_into(image, halo - keep, both_halves(offsets_ref[...]), out_ref)


def merge_into(image, mine, other, weights_ref, level):
    width = mine.shape[1] // 2
    child = lax.shift_right_logical(lax.axis_index("pulse"), level) & 1
    real, imag = [], []
    for block, which in ((mine, child), (other, 1 - child)):
        real_weight = weights_ref[which, 0]
        imag_weight = weights_ref[which, 1]
        re, im = block[:, :width], block[:, width:]
        real.append(mm(re, real_weight) - mm(im, imag_weight))
        imag.append(mm(re, imag_weight) + mm(im, real_weight))
    image[:, :width] = (real[0] + real[1]).astype(image.dtype)
    image[:, width:] = (imag[0] + imag[1]).astype(image.dtype)


def middle_kernel(level, edges, halo, mine, other, weights_ref, offsets_ref, *rest):
    out_ref, image = rest[-2:]
    merge_into(image, mine, other, weights_ref, level)
    mask_outside(image, halo if "left" in edges else 0, halo if "right" in edges else 0)
    shift_into(image, MAXOFF, both_halves(offsets_ref[...]), out_ref)


def last_kernel(level, start, mine, other, weights_ref, *rest):
    out_ref, block, sem = rest[-3:]
    merge_into(block, mine, other, weights_ref, level)
    copy = pltpu.make_async_copy(block, out_ref.at[pl.ds(start, block.shape[0]), :], sem)
    copy.start()
    copy.wait()


VMEM = pl.BlockSpec(memory_space=pltpu.VMEM)
ANY = pl.BlockSpec(memory_space=pl.ANY)


def cost(flops, moved):
    return pl.CostEstimate(flops=flops, bytes_accessed=moved, transcendentals=0)


def exchange(value, axis, level):
    devices = range(lax.axis_size(axis))
    return lax.ppermute(value, axis, [(i, i ^ (1 << level)) for i in devices])


def moved_along(block, axis, distance):
    devices = range(lax.axis_size(axis))
    return lax.ppermute(block, axis, [(i, i + distance) for i in devices if i + distance in devices])


def chunk_plan(rows):
    unit = rows // 8
    edges = [(2, 3), (3, 5), (5, 7), (7, 8), (0, 2)]
    return [(a * unit, b * unit) for a, b in edges]


def body(echoes, chirp, beam_weights, merge_weights, range_offsets):
    taps = chirp.shape[1]
    rows = echoes.shape[2]
    pulses = echoes.shape[1]
    wide = beam_weights.shape[1]
    levels = lax.axis_size("pulse").bit_length() - 1
    plan = chunk_plan(rows)
    halo = -(-MAXOFF * levels // 16) * 16
    band, turned = prepare(chirp, beam_weights)
    offsets = [range_offsets[level : level + 1] for level in range(levels)]
    weights = [merge_weights[level] for level in range(levels)]
    before = moved_along(echoes[:, :, rows - taps :], "range", 1)
    after = moved_along(echoes[:, :, : 2 * taps], "range", -1)

    def sides(start, end):
        return (("left",) if start == 0 else ()) + (("right",) if end == rows else ())

    def first(start, end):
        edges = sides(start, end)
        sources, pieces = [echoes], []
        low, high = start - taps, end + 2 * taps
        if low < 0:
            pieces.append((len(sources), 0, taps))
            sources.append(before)
            low = 0
        pieces.append((0, low, min(high, rows) - low))
        if high > rows:
            pieces.append((len(sources), 0, high - rows))
            sources.append(after)
        keep = MAXOFF * (levels - 1)
        lanes = end - start + 3 * taps
        count = end - start + 2 * halo
        out_rows = end - start + 2 * keep
        kernel = functools.partial(first_kernel, pieces, count, halo, keep, edges)
        return pl.pallas_call(
            kernel,
            out_shape=jax.ShapeDtypeStruct((out_rows, wide), BF16),
            in_specs=[ANY] * len(sources) + [VMEM] * 3,
            out_specs=VMEM,
            scratch_shapes=[
                pltpu.VMEM((2, pulses, lanes), BF16),
                pltpu.VMEM((wide, lanes), BF16),
                pltpu.VMEM((count, wide), F32),
                pltpu.SemaphoreType.DMA((3,)),
            ],
            cost_estimate=cost(2 * lanes * wide * 2 * pulses + 8 * count * taps * wide, 4 * wide * lanes),
            name=f"first_{start}",
        )(*sources, band, turned, offsets[0])

    def middle(level, start, end, mine, other):
        edges = sides(start, end)
        around = MAXOFF * (levels - 1 - level)
        count = end - start + 2 * around
        kernel = functools.partial(middle_kernel, level, edges, around)
        return pl.pallas_call(
            kernel,
            out_shape=jax.ShapeDtypeStruct((count - 2 * MAXOFF, wide), BF16),
            in_specs=[VMEM] * 4,
            out_specs=VMEM,
            scratch_shapes=[pltpu.VMEM((count, wide), F32)],
            cost_estimate=cost(4 * count * wide * wide, 6 * count * wide + 4 * wide * wide),
            name=f"middle_{level}_{start}",
        )(mine, other, weights[level], offsets[level + 1])

    def last(start, end, mine, other, out):
        count = end - start
        level = levels - 1
        arguments = [mine, other, weights[level]]
        specs = [VMEM] * 3
        aliases = {}
        if out is not None:
            arguments.append(out)
            specs.append(ANY)
            aliases = {3: 0}
        return pl.pallas_call(
            functools.partial(last_kernel, level, start),
            out_shape=jax.ShapeDtypeStruct((rows, wide), BF16),
            in_specs=specs,
            out_specs=ANY,
            scratch_shapes=[pltpu.VMEM((count, wide), BF16), pltpu.SemaphoreType.DMA],
            input_output_aliases=aliases,
            cost_estimate=cost(4 * count * wide * wide, 6 * count * wide + 4 * wide * wide),
            name=f"last_{start}",
        )(*arguments)

    blocks = []
    for start, end in plan:
        mine = first(start, end)
        for level in range(levels - 1):
            mine = middle(level, start, end, mine, exchange(mine, "pulse", level))
        blocks.append((start, end, mine, exchange(mine, "pulse", levels - 1)))
    out = None
    for start, end, mine, other in blocks:
        out = last(start, end, mine, other, out)
    return out


def solution(mesh):
    in_specs = (
        P(None, "pulse", "range"),
        P(),
        P("pulse", None),
        P(None, None, None, "pulse", None),
        P(None, "pulse"),
    )
    out_specs = P("range", "pulse")
    return jax.shard_map(body, mesh=mesh, in_specs=in_specs, out_specs=out_specs, check_vma=False)
```

```python
import functools

import jax
import jax.numpy as jnp
from jax import lax
from jax.experimental import pallas as pl
from jax.experimental.pallas import tpu as pltpu
from jax.sharding import PartitionSpec as P

MAXOFF = 8
F32 = jnp.float32
BF16 = jnp.bfloat16


def mm(a, b):
    return lax.dot_general(a, b, (((1,), (0,)), ((), ())), preferred_element_type=F32)


def mm_nt(a, b):
    return lax.dot_general(a, b, (((1,), (1,)), ((), ())), preferred_element_type=F32)


def mask_outside(x_ref, left, right):
    rows = x_ref.shape[0]
    if left:
        keep = jnp.full((left, x_ref.shape[1]), lax.axis_index("range"), jnp.int32) > 0
        x_ref[:left, :] = jnp.where(keep, x_ref[:left, :], 0.0)
    if right:
        last = lax.axis_size("range") - 1
        keep = jnp.full((right, x_ref.shape[1]), lax.axis_index("range"), jnp.int32) < last
        x_ref[rows - right :, :] = jnp.where(keep, x_ref[rows - right :, :], 0.0)


def shift_into(x_ref, first, offsets, out_ref):
    rows, width = out_ref.shape
    spot = lax.broadcasted_iota(jnp.int32, (8, width), 0) + MAXOFF + offsets
    index = spot & 7
    low, high = spot < 8, spot >= 16

    def turned(start):
        tile = x_ref[pl.ds(pl.multiple_of(start, 8), 8), :]
        return jnp.take_along_axis(tile, index, axis=0, mode="promise_in_bounds")

    def step(j, held):
        a, b = held
        base = first + 8 + j * 16
        c, d = turned(base), turned(base + 8)
        upper = jnp.where(low, a, jnp.where(high, c, b))
        lower = jnp.where(low, b, jnp.where(high, d, c))
        out = jnp.concatenate([upper, lower], axis=0).astype(BF16)
        out_ref[pl.ds(pl.multiple_of(j * 16, 16), 16), :] = out
        return c, d

    lax.fori_loop(0, rows // 16, step, (turned(first - 8), turned(first)), unroll=2)


def both_halves(row):
    return jnp.concatenate([row, row], axis=1)


def prepare(chirp_ref, weights_ref, band_ref, turned_ref):
    taps = chirp_ref.shape[1]
    row = lax.broadcasted_iota(jnp.int32, (taps, 2 * taps), 0)
    for part in range(2):
        line = chirp_ref[part : part + 1, :].astype(F32)
        line = jnp.concatenate([line, jnp.zeros_like(line)], axis=1)
        band = jnp.broadcast_to(line, (taps, 2 * taps))
        apart = 1
        while apart < taps:
            band = jnp.where((row & apart) != 0, pltpu.roll(band, apart, 1), band)
            apart *= 2
        band_ref[part * taps : (part + 1) * taps, :] = band.astype(BF16)
    turned_ref[...] = weights_ref[...].astype(F32).T.astype(BF16)


def first_block(pieces, halo, keep, edges, sources, band_ref, weights_ref, offsets_ref, out_ref, beams, image):
    width = weights_ref.shape[0] // 2
    taps = band_ref.shape[0] // 2
    at = 0
    for source, start, count in pieces:
        lanes = slice(start, start + count)
        on_real = mm(weights_ref[...], sources[source][0, :, lanes])
        on_imag = mm(weights_ref[...], sources[source][1, :, lanes])
        beams[:width, at : at + count] = (on_real[:width] - on_imag[width:]).astype(BF16)
        beams[width:, at : at + count] = (on_real[width:] + on_imag[:width]).astype(BF16)
        at += count
    spans = block_spans(image.shape[0], halo, taps)
    at = 0
    for lane, row, count in spans:
        band = jnp.concatenate([band_ref[row : row + count, :], band_ref[taps + row : taps + row + count, :]], axis=0)
        real = mm_nt(band, beams[:width, lane : lane + 2 * taps])
        imag = mm_nt(band, beams[width:, lane : lane + 2 * taps])
        image[at : at + count, :width] = real[:count] + imag[count:]
        image[at : at + count, width:] = imag[:count] - real[count:]
        at += count
    mask_outside(image, halo if "left" in edges else 0, halo if "right" in edges else 0)
    shift_into(image, halo - keep, both_halves(offsets_ref[0:1, :]), out_ref)


def block_spans(rows, halo, taps):
    spans, at = [(0, taps - halo, halo)], halo
    while at < rows:
        count = min(taps, rows - at)
        spans.append((at - halo + taps, 0, count))
        at += count
    return spans


def opening_kernel(pieces, halo, keep, echoes, chirp_ref, steering_ref, offsets_ref, out_ref, band_ref, turned_ref, beams, image):
    prepare(chirp_ref, steering_ref, band_ref, turned_ref)
    first_block(pieces, halo, keep, (), [echoes], band_ref, turned_ref, offsets_ref, out_ref, beams, image)


def first_kernel(pieces, halo, keep, edges, *refs):
    band_ref, turned_ref, offsets_ref, _, out_ref, beams, image = refs[-7:]
    first_block(pieces, halo, keep, edges, refs[:-7], band_ref, turned_ref, offsets_ref, out_ref, beams, image)


def merge_into(image, mine, other, weights_ref, level):
    width = mine.shape[1] // 2
    child = lax.shift_right_logical(lax.axis_index("pulse"), level) & 1
    real, imag = [], []
    for block, which in ((mine, child), (other, 1 - child)):
        real_weight = weights_ref[level, which, 0]
        imag_weight = weights_ref[level, which, 1]
        re, im = block[:, :width], block[:, width:]
        real.append(mm(re, real_weight) - mm(im, imag_weight))
        imag.append(mm(re, imag_weight) + mm(im, real_weight))
    image[:, :width] = (real[0] + real[1]).astype(image.dtype)
    image[:, width:] = (imag[0] + imag[1]).astype(image.dtype)


def middle_kernel(level, edges, halo, mine, other, weights_ref, offsets_ref, _, out_ref, image):
    merge_into(image, mine, other, weights_ref, level)
    mask_outside(image, halo if "left" in edges else 0, halo if "right" in edges else 0)
    shift_into(image, MAXOFF, both_halves(offsets_ref[level + 1 : level + 2, :]), out_ref)


def last_kernel(level, start, mine, other, weights_ref, *rest):
    out_ref, block, sem = rest[-3:]
    merge_into(block, mine, other, weights_ref, level)
    copy = pltpu.make_async_copy(block, out_ref.at[pl.ds(start, block.shape[0]), :], sem)
    copy.start()
    copy.wait()


def rims_kernel(echoes, _, first_ref, last_ref):
    first_ref[...] = echoes[:, :, : first_ref.shape[2]]
    last_ref[...] = echoes[:, :, echoes.shape[2] - last_ref.shape[2] :]


VMEM = pl.BlockSpec(memory_space=pltpu.VMEM)
ANY = pl.BlockSpec(memory_space=pl.ANY)
GRANT = 12 * 2**20


def cost(flops, moved):
    return pl.CostEstimate(flops=flops, bytes_accessed=moved, transcendentals=0)


def inside(value):
    return pltpu.with_memory_space_constraint(value, pltpu.VMEM)


def kept(*shape):
    return pltpu.VMEM(shape, BF16)


def exchange(value, axis, level):
    devices = range(lax.axis_size(axis))
    return inside(lax.ppermute(value, axis, [(i, i ^ (1 << level)) for i in devices]))


def moved_along(block, axis, distance):
    devices = range(lax.axis_size(axis))
    pairs = [(i, i + distance) for i in devices if i + distance in devices]
    return inside(lax.ppermute(block, axis, pairs))


def chunk_plan(rows):
    unit = rows // 8
    edges = [(2, 3), (3, 5), (5, 6), (6, 8), (0, 2)]
    return [(a * unit, b * unit) for a, b in edges]


def work_order(chunks, levels):
    order = [(0, 0), (1, 0), (0, 1), (1, 1)]
    order += [(0, 2), (None, 0), (1, 2), (2, 0), (3, 0), (2, 1), (3, 1), (4, 0), (2, 2), (4, 1), (3, 2), (4, 2)]
    for stage in range(3, levels):
        order += [(chunk, stage) for chunk in range(chunks)]
    return order + [(chunk, levels) for chunk in range(chunks)]


def body(echoes, chirp, beam_weights, merge_weights, range_offsets):
    taps = chirp.shape[1]
    rows = echoes.shape[2]
    wide = beam_weights.shape[1]
    pulses = echoes.shape[1]
    levels = lax.axis_size("pulse").bit_length() - 1
    plan = chunk_plan(rows)
    halo = -(-MAXOFF * levels // 16) * 16
    keep = MAXOFF * (levels - 1)
    params = pltpu.CompilerParams(vmem_limit_bytes=GRANT)
    echoes, merge_weights = inside(echoes), inside(merge_weights)
    chirp, beam_weights, offsets = inside(chirp), inside(beam_weights), inside(range_offsets)
    rims = {}
    prepared = []
    token = None

    def sides(start, end):
        return (("left",) if start == 0 else ()) + (("right",) if end == rows else ())

    def first(start, end):
        sources, pieces = [echoes], []
        low, high = start - taps, end + 2 * taps
        if low < 0:
            pieces.append((len(sources), 0, taps))
            sources.append(rims["before"])
            low = 0
        pieces.append((0, low, min(high, rows) - low))
        if high > rows:
            pieces.append((len(sources), 0, high - rows))
            sources.append(rims["after"])
        lanes = end - start + 3 * taps
        count = end - start + 2 * halo
        out = kept(end - start + 2 * keep, wide)
        scratch = [pltpu.VMEM((wide, lanes), BF16), pltpu.VMEM((count, wide), F32)]
        price = cost(4 * lanes * wide * pulses + 8 * count * taps * wide, 4 * wide * lanes)
        if not prepared:
            result, *made = pl.pallas_call(
                functools.partial(opening_kernel, pieces, halo, keep),
                out_shape=(out, kept(2 * taps, 2 * taps), kept(wide, pulses)),
                in_specs=[VMEM] * 4,
                out_specs=(VMEM,) * 3,
                scratch_shapes=scratch,
                compiler_params=params,
                cost_estimate=price,
            )(echoes, chirp, beam_weights, offsets)
            prepared.extend(inside(m) for m in made)
            return inside(result)
        return inside(
            pl.pallas_call(
                functools.partial(first_kernel, pieces, halo, keep, sides(start, end)),
                out_shape=out,
                in_specs=[VMEM] * (len(sources) + 3) + [ANY],
                out_specs=VMEM,
                scratch_shapes=scratch,
                compiler_params=params,
                cost_estimate=price,
            )(*sources, *prepared, offsets, token)
        )

    def middle(level, start, end, mine, other):
        around = MAXOFF * (levels - 1 - level)
        count = end - start + 2 * around
        return inside(
            pl.pallas_call(
                functools.partial(middle_kernel, level, sides(start, end), around),
                out_shape=kept(count - 2 * MAXOFF, wide),
                in_specs=[VMEM] * 4 + [ANY],
                out_specs=VMEM,
                scratch_shapes=[pltpu.VMEM((count, wide), F32)],
                compiler_params=params,
                cost_estimate=cost(4 * count * wide * wide, 6 * count * wide + 4 * wide * wide),
            )(mine, other, merge_weights, offsets, token)
        )

    def last(start, end, mine, other, out):
        count = end - start
        extra = [token] if out is None else [out]
        return pl.pallas_call(
            functools.partial(last_kernel, levels - 1, start),
            out_shape=jax.ShapeDtypeStruct((rows, wide), BF16),
            in_specs=[VMEM] * 3 + [ANY],
            out_specs=ANY,
            scratch_shapes=[pltpu.VMEM((count, wide), BF16), pltpu.SemaphoreType.DMA],
            input_output_aliases={} if out is None else {3: 0},
            compiler_params=params,
            cost_estimate=cost(4 * count * wide * wide, 6 * count * wide + 4 * wide * wide),
        )(mine, other, merge_weights, *extra)

    def rims_of():
        ends = pl.pallas_call(
            rims_kernel,
            out_shape=(kept(2, pulses, 2 * taps), kept(2, pulses, taps)),
            in_specs=[VMEM, ANY],
            out_specs=(VMEM,) * 2,
            compiler_params=params,
            cost_estimate=cost(0, 12 * pulses * taps),
            name="rims",
        )(echoes, token)
        return [inside(end) for end in ends]

    mine, other, out = {}, {}, None
    for chunk, stage in work_order(len(plan), levels):
        if chunk is None:
            heads, tails = rims_of()
            rims["after"] = moved_along(heads, "range", -1)
            rims["before"] = moved_along(tails, "range", 1)
            token = heads
            continue
        start, end = plan[chunk]
        if stage == levels:
            out = last(start, end, mine[chunk], other[chunk], out)
            continue
        if stage == 0:
            value = first(start, end)
        else:
            value = middle(stage - 1, start, end, mine[chunk], other[chunk])
        token = mine[chunk] = value
        other[chunk] = exchange(value, "pulse", stage)
    return out


def solution(mesh):
    in_specs = (
        P(None, "pulse", "range"),
        P(),
        P("pulse", None),
        P(None, None, None, "pulse", None),
        P(None, "pulse"),
    )
    out_specs = P("range", "pulse")

    return jax.shard_map(body, mesh=mesh, in_specs=in_specs, out_specs=out_specs, check_vma=False)
```

```python
import functools

import jax
import jax.numpy as jnp
from jax import lax
from jax.experimental import pallas as pl
from jax.experimental.pallas import tpu as pltpu
from jax.sharding import PartitionSpec as P

MAXOFF = 8
F32 = jnp.float32
BF16 = jnp.bfloat16


def mm(a, b):
    return lax.dot_general(a, b, (((1,), (0,)), ((), ())), preferred_element_type=F32)


def mm_nt(a, b):
    return lax.dot_general(a, b, (((1,), (1,)), ((), ())), preferred_element_type=F32)


def mask_outside(x_ref, left, right):
    rows = x_ref.shape[0]
    if left:
        keep = jnp.full((left, x_ref.shape[1]), lax.axis_index("range"), jnp.int32) > 0
        x_ref[:left, :] = jnp.where(keep, x_ref[:left, :], 0.0)
    if right:
        last = lax.axis_size("range") - 1
        keep = jnp.full((right, x_ref.shape[1]), lax.axis_index("range"), jnp.int32) < last
        x_ref[rows - right :, :] = jnp.where(keep, x_ref[rows - right :, :], 0.0)


def shift_into(x_ref, first, offsets, out_ref):
    rows, width = out_ref.shape
    spot = lax.broadcasted_iota(jnp.int32, (8, width), 0) + MAXOFF + offsets
    index = spot & 7
    low, high = spot < 8, spot >= 16

    def turned(start):
        tile = x_ref[pl.ds(pl.multiple_of(start, 8), 8), :]
        return jnp.take_along_axis(tile, index, axis=0, mode="promise_in_bounds")

    def step(j, held):
        a, b = held
        base = first + 8 + j * 16
        c, d = turned(base), turned(base + 8)
        upper = jnp.where(low, a, jnp.where(high, c, b))
        lower = jnp.where(low, b, jnp.where(high, d, c))
        out = jnp.concatenate([upper, lower], axis=0).astype(BF16)
        out_ref[pl.ds(pl.multiple_of(j * 16, 16), 16), :] = out
        return c, d

    lax.fori_loop(0, rows // 16, step, (turned(first - 8), turned(first)), unroll=2)


def both_halves(row):
    return jnp.concatenate([row, row], axis=1)


def prepare(chirp_ref, weights_ref, band_ref, turned_ref):
    taps = chirp_ref.shape[1]
    row = lax.broadcasted_iota(jnp.int32, (taps, 2 * taps), 0)
    for part in range(2):
        line = chirp_ref[part : part + 1, :].astype(F32)
        line = jnp.concatenate([line, jnp.zeros_like(line)], axis=1)
        band = jnp.broadcast_to(line, (taps, 2 * taps))
        apart = 1
        while apart < taps:
            band = jnp.where((row & apart) != 0, pltpu.roll(band, apart, 1), band)
            apart *= 2
        band_ref[part * taps : (part + 1) * taps, :] = band.astype(BF16)
    turned_ref[...] = weights_ref[...].astype(F32).T.astype(BF16)


def first_block(pieces, halo, keep, edges, sources, band_ref, weights_ref, offsets_ref, out_ref, beams, image):
    width = weights_ref.shape[0] // 2
    taps = band_ref.shape[0] // 2
    at = 0
    for source, start, count in pieces:
        lanes = slice(start, start + count)
        on_real = mm(weights_ref[...], sources[source][0, :, lanes])
        on_imag = mm(weights_ref[...], sources[source][1, :, lanes])
        beams[:width, at : at + count] = (on_real[:width] - on_imag[width:]).astype(BF16)
        beams[width:, at : at + count] = (on_real[width:] + on_imag[:width]).astype(BF16)
        at += count
    spans = block_spans(image.shape[0], halo, taps)
    at = 0
    for lane, row, count in spans:
        band = jnp.concatenate([band_ref[row : row + count, :], band_ref[taps + row : taps + row + count, :]], axis=0)
        real = mm_nt(band, beams[:width, lane : lane + 2 * taps])
        imag = mm_nt(band, beams[width:, lane : lane + 2 * taps])
        image[at : at + count, :width] = real[:count] + imag[count:]
        image[at : at + count, width:] = imag[:count] - real[count:]
        at += count
    mask_outside(image, halo if "left" in edges else 0, halo if "right" in edges else 0)
    shift_into(image, halo - keep, both_halves(offsets_ref[0:1, :]), out_ref)


def block_spans(rows, halo, taps):
    spans, at = [(0, taps - halo, halo)], halo
    while at < rows:
        count = min(taps, rows - at)
        spans.append((at - halo + taps, 0, count))
        at += count
    return spans


def opening_kernel(lanes, halo, keep, *refs):
    arguments, (out_ref, band_ref, turned_ref, offsets), scratch = refs[:4], refs[4:8], refs[8:]
    echo, chirp, steering, beams, image, sems = scratch
    sources = (arguments[0].at[:, :, pl.ds(*lanes)],) + arguments[1:]
    copies = [
        pltpu.make_async_copy(source, target, sems.at[n])
        for n, (source, target) in enumerate(zip(sources, (echo, chirp, steering, offsets)))
    ]
    for copy in copies:
        copy.start()
    for n in (1, 2):
        copies[n].wait()
    prepare(chirp, steering, band_ref, turned_ref)
    for n in (3, 0):
        copies[n].wait()
    pieces = [(0, 0, lanes[1])]
    first_block(pieces, halo, keep, (), [echo], band_ref, turned_ref, offsets, out_ref, beams, image)


def first_kernel(pieces, halo, keep, edges, *refs):
    band_ref, turned_ref, offsets_ref, _, out_ref, beams, image = refs[-7:]
    first_block(pieces, halo, keep, edges, refs[:-7], band_ref, turned_ref, offsets_ref, out_ref, beams, image)


def merge_into(image, mine, other, weights_ref, level):
    width = mine.shape[1] // 2
    child = lax.shift_right_logical(lax.axis_index("pulse"), level) & 1
    real, imag = [], []
    for block, which in ((mine, child), (other, 1 - child)):
        real_weight = weights_ref[level, which, 0]
        imag_weight = weights_ref[level, which, 1]
        re, im = block[:, :width], block[:, width:]
        real.append(mm(re, real_weight) - mm(im, imag_weight))
        imag.append(mm(re, imag_weight) + mm(im, real_weight))
    image[:, :width] = (real[0] + real[1]).astype(image.dtype)
    image[:, width:] = (imag[0] + imag[1]).astype(image.dtype)


def middle_kernel(level, edges, halo, mine, other, weights_ref, offsets_ref, _, out_ref, image):
    merge_into(image, mine, other, weights_ref, level)
    mask_outside(image, halo if "left" in edges else 0, halo if "right" in edges else 0)
    shift_into(image, MAXOFF, both_halves(offsets_ref[level + 1 : level + 2, :]), out_ref)


def last_kernel(level, start, mine, other, weights_ref, *rest):
    out_ref, block, sem = rest[-3:]
    merge_into(block, mine, other, weights_ref, level)
    copy = pltpu.make_async_copy(block, out_ref.at[pl.ds(start, block.shape[0]), :], sem)
    copy.start()
    copy.wait()


def rims_kernel(echoes, _, first_ref, last_ref):
    first_ref[...] = echoes[:, :, : first_ref.shape[2]]
    last_ref[...] = echoes[:, :, echoes.shape[2] - last_ref.shape[2] :]


VMEM = pl.BlockSpec(memory_space=pltpu.VMEM)
ANY = pl.BlockSpec(memory_space=pl.ANY)
GRANT = 12 * 2**20


def cost(flops, moved):
    return pl.CostEstimate(flops=flops, bytes_accessed=moved, transcendentals=0)


def inside(value):
    return pltpu.with_memory_space_constraint(value, pltpu.VMEM)


def kept(*shape):
    return pltpu.VMEM(shape, BF16)


def exchange(value, axis, level):
    devices = range(lax.axis_size(axis))
    return inside(lax.ppermute(value, axis, [(i, i ^ (1 << level)) for i in devices]))


def moved_along(block, axis, distance):
    devices = range(lax.axis_size(axis))
    pairs = [(i, i + distance) for i in devices if i + distance in devices]
    return inside(lax.ppermute(block, axis, pairs))


def chunk_plan(rows):
    unit = rows // 8
    edges = [(2, 3), (3, 4), (4, 6), (6, 8), (0, 2)]
    return [(a * unit, b * unit) for a, b in edges]


def work_order(chunks, levels):
    order = [(0, 0), (1, 0), (0, 1), (1, 1), (2, 0), (0, 2), (2, 1), (1, 2), (None, 0)]
    order += [(2, 2), (3, 0), (3, 1), (4, 0), (4, 1), (3, 2), (4, 2)]
    for stage in range(3, levels):
        order += [(chunk, stage) for chunk in range(chunks)]
    return order + [(chunk, levels) for chunk in range(chunks)]


def body(echoes, chirp, beam_weights, merge_weights, range_offsets):
    taps = chirp.shape[1]
    rows = echoes.shape[2]
    wide = beam_weights.shape[1]
    pulses = echoes.shape[1]
    levels = lax.axis_size("pulse").bit_length() - 1
    plan = chunk_plan(rows)
    halo = -(-MAXOFF * levels // 16) * 16
    keep = MAXOFF * (levels - 1)
    params = pltpu.CompilerParams(vmem_limit_bytes=GRANT)
    given = [pltpu.with_memory_space_constraint(a, pltpu.HBM) for a in (echoes, chirp, beam_weights, range_offsets)]
    echoes, merge_weights = inside(echoes), inside(merge_weights)
    rims = {}
    prepared = []
    token = None

    def sides(start, end):
        return (("left",) if start == 0 else ()) + (("right",) if end == rows else ())

    def first(start, end):
        sources, pieces = [echoes], []
        low, high = start - taps, end + 2 * taps
        if low < 0:
            pieces.append((len(sources), 0, taps))
            sources.append(rims["before"])
            low = 0
        pieces.append((0, low, min(high, rows) - low))
        if high > rows:
            pieces.append((len(sources), 0, high - rows))
            sources.append(rims["after"])
        lanes = end - start + 3 * taps
        count = end - start + 2 * halo
        out = kept(end - start + 2 * keep, wide)
        scratch = [pltpu.VMEM((wide, lanes), BF16), pltpu.VMEM((count, wide), F32)]
        price = cost(4 * lanes * wide * pulses + 8 * count * taps * wide, 4 * wide * lanes)
        if not prepared:
            result, *made = pl.pallas_call(
                functools.partial(opening_kernel, pieces[0][1:], halo, keep),
                out_shape=(out, kept(2 * taps, 2 * taps), kept(wide, pulses), pltpu.VMEM(range_offsets.shape, jnp.int32)),
                in_specs=[ANY] * 4,
                out_specs=(VMEM,) * 4,
                scratch_shapes=[
                    pltpu.VMEM((2, pulses, lanes), BF16),
                    pltpu.VMEM(chirp.shape, BF16),
                    pltpu.VMEM(beam_weights.shape, BF16),
                    *scratch,
                    pltpu.SemaphoreType.DMA((4,)),
                ],
                compiler_params=params,
                cost_estimate=price,
            )(*given)
            prepared.extend(inside(m) for m in made)
            return inside(result)
        return inside(
            pl.pallas_call(
                functools.partial(first_kernel, pieces, halo, keep, sides(start, end)),
                out_shape=out,
                in_specs=[VMEM] * (len(sources) + 3) + [ANY],
                out_specs=VMEM,
                scratch_shapes=scratch,
                compiler_params=params,
                cost_estimate=price,
            )(*sources, *prepared, token)
        )

    def middle(level, start, end, mine, other):
        around = MAXOFF * (levels - 1 - level)
        count = end - start + 2 * around
        return inside(
            pl.pallas_call(
                functools.partial(middle_kernel, level, sides(start, end), around),
                out_shape=kept(count - 2 * MAXOFF, wide),
                in_specs=[VMEM] * 4 + [ANY],
                out_specs=VMEM,
                scratch_shapes=[pltpu.VMEM((count, wide), F32)],
                compiler_params=params,
                cost_estimate=cost(4 * count * wide * wide, 6 * count * wide + 4 * wide * wide),
            )(mine, other, merge_weights, prepared[-1], token)
        )

    def last(start, end, mine, other, out):
        count = end - start
        extra = [token] if out is None else [out]
        return pl.pallas_call(
            functools.partial(last_kernel, levels - 1, start),
            out_shape=jax.ShapeDtypeStruct((rows, wide), BF16),
            in_specs=[VMEM] * 3 + [ANY],
            out_specs=ANY,
            scratch_shapes=[pltpu.VMEM((count, wide), BF16), pltpu.SemaphoreType.DMA],
            input_output_aliases={} if out is None else {3: 0},
            compiler_params=params,
            cost_estimate=cost(4 * count * wide * wide, 6 * count * wide + 4 * wide * wide),
        )(mine, other, merge_weights, *extra)

    def rims_of():
        ends = pl.pallas_call(
            rims_kernel,
            out_shape=(kept(2, pulses, 2 * taps), kept(2, pulses, taps)),
            in_specs=[VMEM, ANY],
            out_specs=(VMEM,) * 2,
            compiler_params=params,
            cost_estimate=cost(0, 12 * pulses * taps),
            name="rims",
        )(echoes, token)
        return [inside(end) for end in ends]

    mine, other, out = {}, {}, None
    for chunk, stage in work_order(len(plan), levels):
        if chunk is None:
            heads, tails = rims_of()
            rims["after"] = moved_along(heads, "range", -1)
            rims["before"] = moved_along(tails, "range", 1)
            token = heads
            continue
        start, end = plan[chunk]
        if stage == levels:
            out = last(start, end, mine[chunk], other[chunk], out)
            continue
        if stage == 0:
            value = first(start, end)
        else:
            value = middle(stage - 1, start, end, mine[chunk], other[chunk])
        token = mine[chunk] = value
        other[chunk] = exchange(value, "pulse", stage)
    return out


def solution(mesh):
    in_specs = (
        P(None, "pulse", "range"),
        P(),
        P("pulse", None),
        P(None, None, None, "pulse", None),
        P(None, "pulse"),
    )
    out_specs = P("range", "pulse")

    return jax.shard_map(body, mesh=mesh, in_specs=in_specs, out_specs=out_specs, check_vma=False)
```

```python
import functools

import jax
import jax.numpy as jnp
from jax import lax
from jax.experimental import pallas as pl
from jax.experimental.pallas import tpu as pltpu
from jax.sharding import PartitionSpec as P

MAXOFF = 8
F32 = jnp.float32
BF16 = jnp.bfloat16


def mm(a, b):
    return lax.dot_general(a, b, (((1,), (0,)), ((), ())), preferred_element_type=F32)


def mm_nt(a, b):
    return lax.dot_general(a, b, (((1,), (1,)), ((), ())), preferred_element_type=F32)


def mask_outside(x_ref, left, right):
    rows = x_ref.shape[0]
    if left:
        keep = jnp.full((left, x_ref.shape[1]), lax.axis_index("range"), jnp.int32) > 0
        x_ref[:left, :] = jnp.where(keep, x_ref[:left, :], 0.0)
    if right:
        last = lax.axis_size("range") - 1
        keep = jnp.full((right, x_ref.shape[1]), lax.axis_index("range"), jnp.int32) < last
        x_ref[rows - right :, :] = jnp.where(keep, x_ref[rows - right :, :], 0.0)


def shift_into(x_ref, first, offsets, out_ref, at, rows):
    width = out_ref.shape[1]
    spot = lax.broadcasted_iota(jnp.int32, (8, width), 0) + MAXOFF + offsets
    index = spot & 7
    low, high = spot < 8, spot >= 16

    def turned(start):
        tile = x_ref[pl.ds(pl.multiple_of(start, 8), 8), :]
        return jnp.take_along_axis(tile, index, axis=0, mode="promise_in_bounds")

    def step(j, held):
        a, b = held
        base = first + 8 + j * 16
        c, d = turned(base), turned(base + 8)
        upper = jnp.where(low, a, jnp.where(high, c, b))
        lower = jnp.where(low, b, jnp.where(high, d, c))
        out = jnp.concatenate([upper, lower], axis=0).astype(BF16)
        out_ref[pl.ds(pl.multiple_of(at + j * 16, 16), 16), :] = out
        return c, d

    lax.fori_loop(0, rows // 16, step, (turned(first - 8), turned(first)), unroll=2)


def shift_segments(x_ref, around, offsets, out_ref, kept_around, lengths):
    source = target = 0
    for length in lengths:
        rows = length + 2 * kept_around
        shift_into(x_ref, source + around - kept_around, offsets, out_ref, target, rows)
        source += length + 2 * around
        target += rows


def both_halves(row):
    return jnp.concatenate([row, row], axis=1)


def prepare(chirp_ref, weights_ref, band_ref, turned_ref):
    taps = chirp_ref.shape[1]
    for part in range(2):
        line = chirp_ref[part : part + 1, :].astype(F32)
        line = jnp.concatenate([line, jnp.zeros_like(line)], axis=1)
        band = pltpu.roll(jnp.broadcast_to(line, (taps, 2 * taps)), 0, 1, stride=1, stride_axis=0)
        band_ref[part * taps : (part + 1) * taps, :] = band.astype(BF16)
    turned_ref[...] = weights_ref[...].astype(F32).T.astype(BF16)


def first_block(windows, halo, keep, edges, sources, band_ref, weights_ref, offsets_ref, out_ref, beams, image):
    width = weights_ref.shape[0] // 2
    taps = band_ref.shape[0] // 2
    lane = at = 0
    for length, row, pieces in windows:
        base = lane
        for source, start, count in pieces:
            lanes = slice(start, start + count)
            on_real = mm(weights_ref[...], sources[source][0, :, lanes])
            on_imag = mm(weights_ref[...], sources[source][1, :, lanes])
            beams[:width, lane : lane + count] = (on_real[:width] - on_imag[width:]).astype(BF16)
            beams[width:, lane : lane + count] = (on_real[width:] + on_imag[:width]).astype(BF16)
            lane += count
        end = row + length + 2 * halo
        while row < end:
            tile = row // taps * taps
            first, count = row - tile, min(end, tile + taps) - row
            parts = [band_ref[part * taps + first : part * taps + first + count, :] for part in (0, 1)]
            band = jnp.concatenate(parts, axis=0)
            real = mm_nt(band, beams[:width, base + tile : base + tile + 2 * taps])
            imag = mm_nt(band, beams[width:, base + tile : base + tile + 2 * taps])
            image[at : at + count, :width] = real[:count] + imag[count:]
            image[at : at + count, width:] = imag[:count] - real[count:]
            row += count
            at += count
    mask_outside(image, halo if "left" in edges else 0, halo if "right" in edges else 0)
    lengths = [length for length, _, _ in windows]
    shift_segments(image, halo, both_halves(offsets_ref[0:1, :]), out_ref, keep, lengths)


def opening_kernel(window, halo, keep, *refs):
    echoes_in, *small = refs[:4]
    out_ref, echoes, band_ref, turned_ref, offsets = refs[4:9]
    chirp, steering, beams, image, sems = refs[9:]
    lane, lanes = window[2][0][1:]
    spans = [(lane, lanes), (0, lane), (lane + lanes, echoes.shape[2] - lane - lanes)]
    pairs = list(zip(small, (chirp, steering, offsets)))
    for start, count in spans:
        if count:
            part = (slice(None), slice(None), pl.ds(start, count))
            pairs.append((echoes_in.at[part], echoes.at[part]))
    copies = [pltpu.make_async_copy(source, target, sems.at[n]) for n, (source, target) in enumerate(pairs)]
    for copy in copies:
        copy.start()
    for copy in copies[:2]:
        copy.wait()
    prepare(chirp, steering, band_ref, turned_ref)
    for copy in copies[2:4]:
        copy.wait()
    first_block([window], halo, keep, (), [echoes], band_ref, turned_ref, offsets, out_ref, beams, image)
    for copy in copies[4:]:
        copy.wait()


def first_kernel(windows, halo, keep, edges, *refs):
    band_ref, turned_ref, offsets_ref, out_ref, beams, image = refs[-6:]
    first_block(windows, halo, keep, edges, refs[:-6], band_ref, turned_ref, offsets_ref, out_ref, beams, image)


def merge_into(image, mine, other, weights_ref, level):
    width = mine.shape[1] // 2
    child = lax.shift_right_logical(lax.axis_index("pulse"), level) & 1
    real, imag = [], []
    for block, which in ((mine, child), (other, 1 - child)):
        real_weight = weights_ref[level, which, 0]
        imag_weight = weights_ref[level, which, 1]
        re, im = block[:, :width], block[:, width:]
        real.append(mm(re, real_weight) - mm(im, imag_weight))
        imag.append(mm(re, imag_weight) + mm(im, real_weight))
    image[:, :width] = (real[0] + real[1]).astype(image.dtype)
    image[:, width:] = (imag[0] + imag[1]).astype(image.dtype)


def middle_kernel(level, edges, halo, lengths, mine, other, weights_ref, offsets_ref, out_ref, image):
    merge_into(image, mine, other, weights_ref, level)
    mask_outside(image, halo if "left" in edges else 0, halo if "right" in edges else 0)
    offsets = both_halves(offsets_ref[level + 1 : level + 2, :])
    shift_segments(image, halo, offsets, out_ref, halo - MAXOFF, lengths)


def last_kernel(level, segments, mine, other, weights_ref, *rest):
    out_ref, block, sems = rest[-3:]
    merge_into(block, mine, other, weights_ref, level)
    copies, at = [], 0
    for n, (start, end) in enumerate(segments):
        rows = pl.ds(at, end - start)
        copy = pltpu.make_async_copy(block.at[rows, :], out_ref.at[pl.ds(start, end - start), :], sems.at[n])
        copy.start()
        copies.append(copy)
        at += end - start
    for copy in copies:
        copy.wait()


def rims_kernel(echoes, first_ref, last_ref):
    first_ref[...] = echoes[:, :, : first_ref.shape[2]]
    last_ref[...] = echoes[:, :, echoes.shape[2] - last_ref.shape[2] :]


VMEM = pl.BlockSpec(memory_space=pltpu.VMEM)
ANY = pl.BlockSpec(memory_space=pl.ANY)
GRANT = 12 * 2**20


def cost(flops, moved):
    return pl.CostEstimate(flops=flops, bytes_accessed=moved, transcendentals=0)


def inside(value):
    return pltpu.with_memory_space_constraint(value, pltpu.VMEM)


def kept(*shape):
    return pltpu.VMEM(shape, BF16)


def exchange(value, axis, level):
    devices = range(lax.axis_size(axis))
    return inside(lax.ppermute(value, axis, [(i, i ^ (1 << level)) for i in devices]))


def moved_along(block, axis, distance):
    devices = range(lax.axis_size(axis))
    pairs = [(i, i + distance) for i in devices if i + distance in devices]
    return inside(lax.ppermute(block, axis, pairs))


SHARES = (160, 224, 224, 224)
ORDER = (
    *("0a", "1a", "0b", "1b", "2a", "0c", "1c", "0d", "2b", "H", "1d", "2c", "0e", "1e", "2d"),
    *("3a", "2e", "3b", "3c", "3d", "3e"),
)


def chunk_plan(rows, taps, halo):
    start, end = halo, rows - taps - halo
    plan, total, seen = [], sum(SHARES), 0
    for share in SHARES:
        seen += share
        stop = halo + (end - halo) * seen // total // 16 * 16
        plan.append([(start, stop)])
        start = stop
    return plan + [[(0, halo), (end, rows)]]


def work_order(levels):
    chunks = len(SHARES) + 1
    order = [(None, 0) if step == "H" else (ord(step[1]) - ord("a"), int(step[0])) for step in ORDER]
    if levels == 3:
        return order
    order = [(chunk, stage) for chunk, stage in order if stage < min(3, levels)]
    for stage in range(min(3, levels), levels + 1):
        order += [(chunk, stage) for chunk in range(chunks)]
    return order


def body(echoes, chirp, beam_weights, merge_weights, range_offsets):
    taps = chirp.shape[1]
    rows = echoes.shape[2]
    wide = beam_weights.shape[1]
    pulses = echoes.shape[1]
    levels = lax.axis_size("pulse").bit_length() - 1
    halo = -(-MAXOFF * levels // 16) * 16
    plan = chunk_plan(rows, taps, halo)
    keep = MAXOFF * (levels - 1)
    params = pltpu.CompilerParams(vmem_limit_bytes=GRANT)
    given = [pltpu.with_memory_space_constraint(a, pltpu.HBM) for a in (echoes, chirp, beam_weights, range_offsets)]
    merge_weights = inside(merge_weights)
    rims = {}
    prepared = []

    def sides(segments):
        return ("left", "right") if len(segments) > 1 else ()

    def lengths_of(segments):
        return tuple(end - start for start, end in segments)

    def windows_of(segments):
        sources, windows = prepared[:1], []
        if len(segments) > 1:
            sources += [rims["before"], rims["after"]]
        for start, end in segments:
            low = (start - halo) // taps * taps
            high = -(-(end + halo) // taps) * taps + taps
            pieces = []
            if low < 0:
                pieces.append((1, 0, -low))
            pieces.append((0, max(low, 0), min(high, rows) - max(low, 0)))
            if high > rows:
                pieces.append((2, 0, high - rows))
            windows.append((end - start, start - halo - low, pieces))
        return sources, windows

    def first(segments):
        sources, windows = windows_of(segments)
        lengths = lengths_of(segments)
        lanes = sum(count for _, _, pieces in windows for _, _, count in pieces)
        count = sum(length + 2 * halo for length in lengths)
        out = kept(sum(length + 2 * keep for length in lengths), wide)
        scratch = [pltpu.VMEM((wide, lanes), BF16), pltpu.VMEM((count, wide), F32)]
        price = cost(4 * lanes * wide * pulses + 8 * count * taps * wide, 4 * wide * lanes)
        if not prepared:
            shared = (kept(*echoes.shape), kept(2 * taps, 2 * taps), kept(wide, pulses), pltpu.VMEM(range_offsets.shape, jnp.int32))
            result, *made = pl.pallas_call(
                functools.partial(opening_kernel, windows[0], halo, keep),
                out_shape=(out, *shared),
                in_specs=[ANY] * 4,
                out_specs=(VMEM,) * 5,
                scratch_shapes=[
                    pltpu.VMEM(chirp.shape, BF16),
                    pltpu.VMEM(beam_weights.shape, BF16),
                    *scratch,
                    pltpu.SemaphoreType.DMA((6,)),
                ],
                compiler_params=params,
                cost_estimate=price,
            )(*given)
            prepared.extend(inside(m) for m in made)
            return inside(result)
        return inside(
            pl.pallas_call(
                functools.partial(first_kernel, windows, halo, keep, sides(segments)),
                out_shape=out,
                in_specs=[VMEM] * (len(sources) + 3),
                out_specs=VMEM,
                scratch_shapes=scratch,
                compiler_params=params,
                cost_estimate=price,
            )(*sources, *prepared[1:])
        )

    def middle(level, segments, mine, other):
        around = MAXOFF * (levels - 1 - level)
        lengths = lengths_of(segments)
        count = mine.shape[0]
        return inside(
            pl.pallas_call(
                functools.partial(middle_kernel, level, sides(segments), around, lengths),
                out_shape=kept(count - 2 * MAXOFF * len(lengths), wide),
                in_specs=[VMEM] * 4,
                out_specs=VMEM,
                scratch_shapes=[pltpu.VMEM((count, wide), F32)],
                compiler_params=params,
                cost_estimate=cost(4 * count * wide * wide, 6 * count * wide + 4 * wide * wide),
            )(mine, other, merge_weights, prepared[-1])
        )

    def last(segments, mine, other, out):
        count = mine.shape[0]
        extra = [] if out is None else [out]
        return pl.pallas_call(
            functools.partial(last_kernel, levels - 1, segments),
            out_shape=jax.ShapeDtypeStruct((rows, wide), BF16),
            in_specs=[VMEM] * 3 + [ANY] * len(extra),
            out_specs=ANY,
            scratch_shapes=[pltpu.VMEM((count, wide), BF16), pltpu.SemaphoreType.DMA((len(segments),))],
            input_output_aliases={} if out is None else {3: 0},
            compiler_params=params,
            cost_estimate=cost(4 * count * wide * wide, 6 * count * wide + 4 * wide * wide),
        )(mine, other, merge_weights, *extra)

    def rims_of():
        ends = pl.pallas_call(
            rims_kernel,
            out_shape=(kept(2, pulses, 2 * taps), kept(2, pulses, taps)),
            in_specs=[VMEM],
            out_specs=(VMEM,) * 2,
            compiler_params=params,
            cost_estimate=cost(0, 12 * pulses * taps),
            name="rims",
        )(prepared[0])
        return [inside(end) for end in ends]

    mine, other, out = {}, {}, None
    for chunk, stage in work_order(levels):
        if chunk is None:
            heads, tails = rims_of()
            rims["after"] = moved_along(heads, "range", -1)
            rims["before"] = moved_along(tails, "range", 1)
            continue
        segments = plan[chunk]
        if stage == levels:
            out = last(segments, mine[chunk], other[chunk], out)
            continue
        if stage == 0:
            value = first(segments)
        else:
            value = middle(stage - 1, segments, mine[chunk], other[chunk])
        mine[chunk] = value
        other[chunk] = exchange(value, "pulse", stage)
    return out


def solution(mesh):
    in_specs = (
        P(None, "pulse", "range"),
        P(),
        P("pulse", None),
        P(None, None, None, "pulse", None),
        P(None, "pulse"),
    )
    out_specs = P("range", "pulse")

    return jax.shard_map(body, mesh=mesh, in_specs=in_specs, out_specs=out_specs, check_vma=False)
```

```python
import functools

import jax
import jax.numpy as jnp
from jax import lax
from jax.experimental import pallas as pl
from jax.experimental.pallas import tpu as pltpu
from jax.sharding import PartitionSpec as P

MAXOFF = 8
F32 = jnp.float32
BF16 = jnp.bfloat16


def mm(a, b):
    return lax.dot_general(a, b, (((1,), (0,)), ((), ())), preferred_element_type=F32)


def mm_nt(a, b):
    return lax.dot_general(a, b, (((1,), (1,)), ((), ())), preferred_element_type=F32)


def mask_outside(x_ref, left, right):
    rows = x_ref.shape[0]
    if left:
        keep = jnp.full((left, x_ref.shape[1]), lax.axis_index("range"), jnp.int32) > 0
        x_ref[:left, :] = jnp.where(keep, x_ref[:left, :], 0.0)
    if right:
        last = lax.axis_size("range") - 1
        keep = jnp.full((right, x_ref.shape[1]), lax.axis_index("range"), jnp.int32) < last
        x_ref[rows - right :, :] = jnp.where(keep, x_ref[rows - right :, :], 0.0)


def shift_into(x_ref, first, offsets, out_ref, at, rows):
    width = out_ref.shape[1]
    spot = lax.broadcasted_iota(jnp.int32, (8, width), 0) + MAXOFF + offsets
    index = spot & 7
    low, high = spot < 8, spot >= 16

    def turned(start):
        tile = x_ref[pl.ds(pl.multiple_of(start, 8), 8), :]
        return jnp.take_along_axis(tile, index, axis=0, mode="promise_in_bounds")

    def step(j, held):
        a, b = held
        base = first + 8 + j * 16
        c, d = turned(base), turned(base + 8)
        upper = jnp.where(low, a, jnp.where(high, c, b))
        lower = jnp.where(low, b, jnp.where(high, d, c))
        out = jnp.concatenate([upper, lower], axis=0).astype(BF16)
        out_ref[pl.ds(pl.multiple_of(at + j * 16, 16), 16), :] = out
        return c, d

    lax.fori_loop(0, rows // 16, step, (turned(first - 8), turned(first)), unroll=2)


def shift_segments(x_ref, around, offsets, out_ref, kept_around, lengths):
    source = target = 0
    for length in lengths:
        rows = length + 2 * kept_around
        shift_into(x_ref, source + around - kept_around, offsets, out_ref, target, rows)
        source += length + 2 * around
        target += rows


def both_halves(row):
    return jnp.concatenate([row, row], axis=1)


def prepare(chirp_ref, weights_ref, band_ref, turned_ref):
    taps = chirp_ref.shape[1]
    for part in range(2):
        line = chirp_ref[part : part + 1, :].astype(F32)
        line = jnp.concatenate([line, jnp.zeros_like(line)], axis=1)
        band = pltpu.roll(jnp.broadcast_to(line, (taps, 2 * taps)), 0, 1, stride=1, stride_axis=0)
        band_ref[part * taps : (part + 1) * taps, :] = band.astype(BF16)
    turned_ref[...] = weights_ref[...].astype(F32).T.astype(BF16)


def first_block(windows, halo, keep, edges, sources, band_ref, weights_ref, offsets_ref, out_ref, beams, image):
    width = weights_ref.shape[0] // 2
    taps = band_ref.shape[0] // 2
    lane = at = 0
    for length, row, pieces in windows:
        base = lane
        for source, start, count in pieces:
            lanes = slice(start, start + count)
            on_real = mm(weights_ref[...], sources[source][0, :, lanes])
            on_imag = mm(weights_ref[...], sources[source][1, :, lanes])
            beams[:width, lane : lane + count] = (on_real[:width] - on_imag[width:]).astype(BF16)
            beams[width:, lane : lane + count] = (on_real[width:] + on_imag[:width]).astype(BF16)
            lane += count
        end = row + length + 2 * halo
        while row < end:
            tile = row // taps * taps
            first, count = row - tile, min(end, tile + taps) - row
            parts = [band_ref[part * taps + first : part * taps + first + count, :] for part in (0, 1)]
            band = jnp.concatenate(parts, axis=0)
            real = mm_nt(band, beams[:width, base + tile : base + tile + 2 * taps])
            imag = mm_nt(band, beams[width:, base + tile : base + tile + 2 * taps])
            image[at : at + count, :width] = real[:count] + imag[count:]
            image[at : at + count, width:] = imag[:count] - real[count:]
            row += count
            at += count
    mask_outside(image, halo if "left" in edges else 0, halo if "right" in edges else 0)
    lengths = [length for length, _, _ in windows]
    shift_segments(image, halo, both_halves(offsets_ref[0:1, :]), out_ref, keep, lengths)


def opening_kernel(window, halo, keep, *refs):
    echoes_in, weights_in, *small = refs[:5]
    out_ref, echoes, weights, band_ref, turned_ref, offsets = refs[5:11]
    chirp, steering, beams, image, sems = refs[11:]
    lane, lanes = window[2][0][1:]
    spans = [(lane, lanes), (0, lane), (lane + lanes, echoes.shape[2] - lane - lanes)]
    pairs = list(zip(small, (chirp, steering, offsets)))
    for start, count in spans:
        if count:
            part = (slice(None), slice(None), pl.ds(start, count))
            pairs.append((echoes_in.at[part], echoes.at[part]))
    pairs.append((weights_in, weights))
    copies = [pltpu.make_async_copy(source, target, sems.at[n]) for n, (source, target) in enumerate(pairs)]
    for copy in copies:
        copy.start()
    for copy in copies[:2]:
        copy.wait()
    prepare(chirp, steering, band_ref, turned_ref)
    for copy in copies[2:4]:
        copy.wait()
    first_block([window], halo, keep, (), [echoes], band_ref, turned_ref, offsets, out_ref, beams, image)
    for copy in copies[4:]:
        copy.wait()


def first_kernel(windows, halo, keep, edges, *refs):
    band_ref, turned_ref, offsets_ref, out_ref, beams, image = refs[-6:]
    first_block(windows, halo, keep, edges, refs[:-6], band_ref, turned_ref, offsets_ref, out_ref, beams, image)


def merge_into(image, mine, other, weights_ref, level, base=0):
    width = mine.shape[1] // 2
    rows = slice(base, base + image.shape[0])
    child = lax.shift_right_logical(lax.axis_index("pulse"), level) & 1
    real, imag = [], []
    for block, which in ((mine, child), (other, 1 - child)):
        real_weight = weights_ref[level, which, 0]
        imag_weight = weights_ref[level, which, 1]
        re, im = block[rows, :width], block[rows, width:]
        real.append(mm(re, real_weight) - mm(im, imag_weight))
        imag.append(mm(re, imag_weight) + mm(im, real_weight))
    image[:, :width] = (real[0] + real[1]).astype(image.dtype)
    image[:, width:] = (imag[0] + imag[1]).astype(image.dtype)


def middle_kernel(level, edges, halo, lengths, base, mine, other, weights_ref, offsets_ref, out_ref, image):
    merge_into(image, mine, other, weights_ref, level, base)
    mask_outside(image, halo if "left" in edges else 0, halo if "right" in edges else 0)
    offsets = both_halves(offsets_ref[level + 1 : level + 2, :])
    shift_segments(image, halo, offsets, out_ref, halo - MAXOFF, lengths)


def last_kernel(level, segments, mine, other, weights_ref, *rest):
    out_ref, block, sems = rest[-3:]
    merge_into(block, mine, other, weights_ref, level)
    copies, at = [], 0
    for n, (start, end) in enumerate(segments):
        rows = pl.ds(at, end - start)
        copy = pltpu.make_async_copy(block.at[rows, :], out_ref.at[pl.ds(start, end - start), :], sems.at[n])
        copy.start()
        copies.append(copy)
        at += end - start
    for copy in copies:
        copy.wait()


def rims_kernel(echoes, first_ref, last_ref):
    first_ref[...] = echoes[:, :, : first_ref.shape[2]]
    last_ref[...] = echoes[:, :, echoes.shape[2] - last_ref.shape[2] :]


VMEM = pl.BlockSpec(memory_space=pltpu.VMEM)
ANY = pl.BlockSpec(memory_space=pl.ANY)
GRANT = 12 * 2**20


def cost(flops, moved):
    return pl.CostEstimate(flops=flops, bytes_accessed=moved, transcendentals=0)


def inside(value):
    return pltpu.with_memory_space_constraint(value, pltpu.VMEM)


def kept(*shape):
    return pltpu.VMEM(shape, BF16)


def exchange(value, axis, level):
    devices = range(lax.axis_size(axis))
    return inside(lax.ppermute(value, axis, [(i, i ^ (1 << level)) for i in devices]))


def moved_along(block, axis, distance):
    devices = range(lax.axis_size(axis))
    pairs = [(i, i + distance) for i in devices if i + distance in devices]
    return inside(lax.ppermute(block, axis, pairs))


SHARES = (176, 144, 80, 224, 208)
GROUPS = ("a", "b", "cde", "f")
ORDER = (
    *("0a", "0b", "1a", "0c", "1b", "1c", "2a", "1d", "2b", "H", "2c", "1e", "2d", "0f", "1f", "2e"),
    *("3a", "2f", "3b", "3c", "3d", "3e", "3f"),
)


def chunk_plan(rows, taps, halo):
    start, end = halo, rows - taps - halo
    plan, total, seen = [], sum(SHARES), 0
    for share in SHARES:
        seen += share
        stop = halo + (end - halo) * seen // total // 16 * 16
        plan.append([(start, stop)])
        start = stop
    return plan + [[(0, halo), (end, rows)]]


def work_order(levels):
    chunks = len(SHARES) + 1
    order = [(None, 0) if step == "H" else (ord(step[1]) - ord("a"), int(step[0])) for step in ORDER]
    if levels == 3:
        return order
    order = [(chunk, stage) for chunk, stage in order if stage < min(3, levels)]
    for stage in range(min(3, levels), levels + 1):
        order += [(chunk, stage) for chunk in range(chunks)]
    return order


def body(echoes, chirp, beam_weights, merge_weights, range_offsets):
    taps = chirp.shape[1]
    rows = echoes.shape[2]
    wide = beam_weights.shape[1]
    pulses = echoes.shape[1]
    levels = lax.axis_size("pulse").bit_length() - 1
    halo = -(-MAXOFF * levels // 16) * 16
    plan = chunk_plan(rows, taps, halo)
    keep = MAXOFF * (levels - 1)
    params = pltpu.CompilerParams(vmem_limit_bytes=GRANT)
    given = (echoes, merge_weights, chirp, beam_weights, range_offsets)
    given = [pltpu.with_memory_space_constraint(value, pltpu.HBM) for value in given]
    rims = {}
    prepared = []

    def sides(segments):
        return ("left", "right") if len(segments) > 1 else ()

    def lengths_of(segments):
        return tuple(end - start for start, end in segments)

    def windows_of(segments):
        sources, windows = prepared[:1], []
        if len(segments) > 1:
            sources += [rims["before"], rims["after"]]
        for start, end in segments:
            low = (start - halo) // taps * taps
            high = -(-(end + halo) // taps) * taps + taps
            pieces = []
            if low < 0:
                pieces.append((1, 0, -low))
            pieces.append((0, max(low, 0), min(high, rows) - max(low, 0)))
            if high > rows:
                pieces.append((2, 0, high - rows))
            windows.append((end - start, start - halo - low, pieces))
        return sources, windows

    def first(segments):
        sources, windows = windows_of(segments)
        lengths = lengths_of(segments)
        lanes = sum(count for _, _, pieces in windows for _, _, count in pieces)
        count = sum(length + 2 * halo for length in lengths)
        out = kept(sum(length + 2 * keep for length in lengths), wide)
        scratch = [pltpu.VMEM((wide, lanes), BF16), pltpu.VMEM((count, wide), F32)]
        price = cost(4 * lanes * wide * pulses + 8 * count * taps * wide, 4 * wide * lanes)
        if not prepared:
            shared = (kept(*echoes.shape), kept(*merge_weights.shape), kept(2 * taps, 2 * taps), kept(wide, pulses), pltpu.VMEM(range_offsets.shape, jnp.int32))
            result, *made = pl.pallas_call(
                functools.partial(opening_kernel, windows[0], halo, keep),
                out_shape=(out, *shared),
                in_specs=[ANY] * 5,
                out_specs=(VMEM,) * 6,
                scratch_shapes=[
                    pltpu.VMEM(chirp.shape, BF16),
                    pltpu.VMEM(beam_weights.shape, BF16),
                    *scratch,
                    pltpu.SemaphoreType.DMA((7,)),
                ],
                compiler_params=params,
                cost_estimate=price,
            )(*given)
            prepared.extend(inside(m) for m in made)
            return inside(result)
        return inside(
            pl.pallas_call(
                functools.partial(first_kernel, windows, halo, keep, sides(segments)),
                out_shape=out,
                in_specs=[VMEM] * (len(sources) + 3),
                out_specs=VMEM,
                scratch_shapes=scratch,
                compiler_params=params,
                cost_estimate=price,
            )(*sources, *prepared[2:])
        )

    def middle(level, segments, mine, other, base):
        around = MAXOFF * (levels - 1 - level)
        lengths = lengths_of(segments)
        count = sum(length + 2 * around for length in lengths)
        return inside(
            pl.pallas_call(
                functools.partial(middle_kernel, level, sides(segments), around, lengths, base),
                out_shape=kept(count - 2 * MAXOFF * len(lengths), wide),
                in_specs=[VMEM] * 4,
                out_specs=VMEM,
                scratch_shapes=[pltpu.VMEM((count, wide), F32)],
                compiler_params=params,
                cost_estimate=cost(4 * count * wide * wide, 6 * count * wide + 4 * wide * wide),
            )(mine, other, prepared[1], prepared[-1])
        )

    def last(segments, mine, other, out):
        count = mine.shape[0]
        extra = [] if out is None else [out]
        return pl.pallas_call(
            functools.partial(last_kernel, levels - 1, segments),
            out_shape=jax.ShapeDtypeStruct((rows, wide), BF16),
            in_specs=[VMEM] * 3 + [ANY] * len(extra),
            out_specs=ANY,
            scratch_shapes=[pltpu.VMEM((count, wide), BF16), pltpu.SemaphoreType.DMA((len(segments),))],
            input_output_aliases={} if out is None else {3: 0},
            compiler_params=params,
            cost_estimate=cost(4 * count * wide * wide, 6 * count * wide + 4 * wide * wide),
        )(mine, other, prepared[1], *extra)

    def rims_of():
        ends = pl.pallas_call(
            rims_kernel,
            out_shape=(kept(2, pulses, 2 * taps), kept(2, pulses, taps)),
            in_specs=[VMEM],
            out_specs=(VMEM,) * 2,
            compiler_params=params,
            cost_estimate=cost(0, 12 * pulses * taps),
            name="rims",
        )(prepared[0])
        return [inside(end) for end in ends]

    mine, other, base, out = {}, {}, {}, None
    groups = {ord(group[0]) - ord("a"): [ord(letter) - ord("a") for letter in group] for group in GROUPS}
    for chunk, stage in work_order(levels):
        if chunk is None:
            heads, tails = rims_of()
            rims["after"] = moved_along(heads, "range", -1)
            rims["before"] = moved_along(tails, "range", 1)
            continue
        segments = plan[chunk]
        if stage == levels:
            out = last(segments, mine[chunk], other[chunk], out)
            continue
        if stage == 0:
            members = groups[chunk]
            if len(members) > 1:
                segments = [(plan[members[0]][0][0], plan[members[-1]][0][1])]
            value = first(segments)
        else:
            value = middle(stage - 1, segments, mine[chunk], other[chunk], base.get(chunk, 0) if stage == 1 else 0)
        if stage == 0:
            received = exchange(value, "pulse", 0)
            for member in members:
                mine[member], other[member] = value, received
                base[member] = plan[member][0][0] - segments[0][0]
            continue
        mine[chunk] = value
        other[chunk] = exchange(value, "pulse", stage)
    return out


def solution(mesh):
    in_specs = (
        P(None, "pulse", "range"),
        P(),
        P("pulse", None),
        P(None, None, None, "pulse", None),
        P(None, "pulse"),
    )
    out_specs = P("range", "pulse")

    return jax.shard_map(body, mesh=mesh, in_specs=in_specs, out_specs=out_specs, check_vma=False)
```
